256 devices in a mesh: row: 32 (over y_hi, z, core), col: 8 (over y_lo, x).
Axes of the slice: x: 4, y: 4 (y_hi: 2, y_lo: 2; y = y_hi * 2 + y_lo), z: 8, core: 2. Of those that a mesh axis runs over, the one named last changes fastest.
Arguments:
- hamiltonian: float32 [24576, 24576], P('row', 'col'), may hold values from -2 to 2, as said below
- vectors: float32 [24576, 512], P(('row', 'col')), may hold values from -6 to 6
Outputs:
- filtered: float32 [24576, 512], P(('row', 'col'))
The draws below stay inside these ranges and needn't reach their ends.
Inputs may be any that keep to these rules, and one draw needn't show every extreme that they name: `hamiltonian`: exactly symmetric, with a diagonal part and a dense part of comparable weight.
All inputs are finite; a program needn't handle non-finite values.
Results may differ from the reference program's by a relative error of at most 0.0001.
Values sent between devices are 32-bit elements; how exact they have to be, the bound alone decides.
A program may use at most 64 MiB of HBM per device.

```python
import jax
import jax.numpy as jnp
from jax import lax

NV = 512
DEGREE = 2
N = 24576


def draw_hamiltonian(key, part):
    base = jax.random.fold_in(key, 11)
    first, second = jax.random.split(base)
    dense = jnp.clip(jax.random.normal(first, (N, N), jnp.float32), -6.0, 6.0)
    diagonal = jax.random.uniform(second, (N,), jnp.float32, -1.0, 1.0)
    scale = 0.5 / jnp.sqrt(jnp.float32(N))
    return (dense + dense.T) * scale + jnp.diag(diagonal)


def shard_levels(own_key, dims, shards, smallest, high):
    factor_of = 1.0
    for dim, parts in shards:
        heights = jax.random.uniform(jax.random.fold_in(jax.random.fold_in(own_key, 6), dim), (parts,), jnp.float32, smallest / len(shards), high / len(shards))
        factor_of = factor_of * jnp.repeat(jnp.exp(heights), dims[dim] // parts).reshape((-1,) + (1,) * (len(dims) - 1 - dim))
    return factor_of


def gaussian(own_key, dims, scale, most, cuts=(), kind=jnp.bfloat16):
    result = scale * jax.random.normal(own_key, dims, jnp.float32)
    if cuts:
        result = result * shard_levels(own_key, dims, cuts, -0.22, 0.18)
    return jnp.clip(result, -most, most).astype(kind)


def setup_inputs(seed: int = 0) -> dict:
    splits = jax.random.split(jax.random.key(seed), 3)
    hamiltonian = draw_hamiltonian(jax.random.fold_in(splits[2], 71), 0)
    vectors = gaussian(splits[1], (N, NV), 1.0, 6.0, ((0, 256),), jnp.float32)
    return {"hamiltonian": hamiltonian, "vectors": vectors}


center = 0.6
half_width = 1.8


def reference(hamiltonian, vectors):
    def apply_shift(block):
        return jnp.dot(hamiltonian, block, precision=lax.Precision.HIGHEST, preferred_element_type=jnp.float32) - center * block

    older = vectors
    recent = vectors
    for degree in range(1, DEGREE + 1):
        product = apply_shift(recent)
        if degree == 1:
            fresh = product * (1.0 / half_width)
        else:
            fresh = (2.0 / half_width) * product - older
        older = recent
        recent = fresh
    return recent
```

```python
import functools

import jax
import jax.numpy as jnp
from jax import lax
from jax.experimental import pallas as pl
from jax.experimental.pallas import tpu as pltpu
from jax.sharding import PartitionSpec as P

MESH = pl.DeviceIdType.MESH
F32 = jnp.float32
BF16 = jnp.bfloat16

CENTER = 0.6
HALF_WIDTH = 1.8

CHUNKS = 4
WIDE = 128
ROWS, COLS = 768, 3072
HALF = COLS // 2
OWN = 96
PIECES = 8
TILE = 512

READY = (0, 3, 5, 8, 13, 17, 21, 25, 29, 33, 36.5, 40, 43.5, 45, 47, 51, 54, 57)
APART = 8.0


def split(value):
    high = value.astype(BF16)
    return high, (value - high.astype(F32)).astype(BF16)


def kernel(h_ref, v_ref, o_ref, h_in, h_hi, h_lo, y0, cat0, p1, cr, zr, yb, yr, y1, cat1, p2, xr, xb, lr,
           h_sem, send_sem, recv_sem):
    row, col = lax.axis_index("row"), lax.axis_index("col")
    core, z, y_hi = lax.rem(row, 2), lax.rem(row // 2, 8), row // 16
    x, y_lo = lax.rem(col, 4), col // 4

    def at_z(k):
        return lax.rem(z + k, 8)

    def at_x(k):
        return lax.rem(x + k, 4)

    z_up = (y_hi * 16 + at_z(1) * 2 + core, col)
    z_down = (y_hi * 16 + at_z(7) * 2 + core, col)
    sibling = (row + 1 - 2 * core, col)
    y_far = (lax.rem(row + 16, 32), col)
    x_up = (row, y_lo * 4 + at_x(1))
    x_down = (row, y_lo * 4 + at_x(3))
    y_near = (row, lax.rem(col + 4, 8))
    partners = (z_up, z_down, sibling, y_far, x_up, x_down, y_near)

    loads = [
        pltpu.make_async_copy(h_ref.at[pl.ds(OWN * i, OWN), :], h_in.at[i], h_sem.at[i]) for i in range(PIECES)
    ]
    for load in loads:
        load.start()

    barrier = pltpu.get_barrier_semaphore()
    for partner in partners:
        pl.semaphore_signal(barrier, inc=1, device_id=partner, device_id_type=MESH)
    pl.semaphore_wait(barrier, len(partners))

    started = {}

    def send(key, src, dst, device):
        n = len(started)
        copy = pltpu.make_async_remote_copy(
            src_ref=src, dst_ref=dst, send_sem=send_sem.at[n], recv_sem=recv_sem.at[n],
            device_id=device, device_id_type=MESH,
        )
        copy.start()
        started[key] = copy

    def arrived(*key):
        started[key].wait_recv()

    def slot(other, k):
        return (y_lo + other - 2 * other * y_lo) * 4 + at_x(k)

    def lanes(q):
        return pl.ds(WIDE * q, WIDE)

    def gather_0(q):
        y0[q, col] = v_ref[:, lanes(q)]
        own = v_ref.at[:, lanes(q)]
        for n, device in enumerate((y_near, x_up, x_down)):
            send((q, "a", n), own, y0.at[q, col], device)

    def gather_1(q):
        arrived(q, "a", 0)
        other = y0.at[q, slot(1, 0)]
        send((q, "a", 3), other, other, x_up)
        send((q, "a", 4), other, other, x_down)

    def gather_2(q):
        arrived(q, "a", 1)
        piece = y0.at[q, slot(0, 3)]
        send((q, "a", 5), piece, piece, x_up)
        arrived(q, "a", 4)
        piece = y0.at[q, slot(1, 1)]
        send((q, "a", 6), piece, piece, x_down)

    def product_1(q):
        for n in (2, 3, 5, 6):
            arrived(q, "a", n)
        high, low = split(y0[q].reshape(ROWS, WIDE).T)
        cat0[0:WIDE, :] = high
        cat0[WIDE:, :] = low

        def half_of(half):
            def step(j, carry):
                at = pl.multiple_of(half * HALF + j * TILE, 128)
                both = jnp.dot(cat0[...], h_hi[:, pl.ds(at, TILE)], preferred_element_type=F32)
                rest = jnp.dot(cat0[0:WIDE, :], h_lo[:, pl.ds(at, TILE)], preferred_element_type=F32)
                value = both[:WIDE] + (both[WIDE:] + rest)
                p1[q, half, :, :, pl.ds(pl.multiple_of(j * TILE, 128), TILE)] = value.reshape(8, 16, TILE)
                return carry

            lax.fori_loop(0, HALF // TILE, step, 0)

        half_of(1 - core)
        send((q, "c"), p1.at[q, 1 - core], cr.at[q], sibling)
        half_of(core)

    def scatter_0(q):
        arrived(q, "c")
        far = at_z(4)
        p1[q, core, far] = p1[q, core, far] + cr[q, far]
        send((q, "r", 0, 1), p1.at[q, core, far, pl.ds(0, 8)], zr.at[q, 0, 0, pl.ds(0, 8)], z_up)
        send((q, "r", 1, 1), p1.at[q, core, far, pl.ds(8, 8)], zr.at[q, 1, 0, pl.ds(8, 8)], z_down)

    def scatter(step, q):
        for way, device in ((0, z_up), (1, z_down)):
            to = at_z(5 - step) if way == 0 else at_z(3 + step)
            arrived(q, "r", way, step - 1)
            if step == 2:
                first, second = pl.ds(8 * way, 8), pl.ds(8 - 8 * way, 8)
                p1[q, core, to, first] = p1[q, core, to, first] + cr[q, to, first] + zr[q, way, 0, first]
                p1[q, core, to, second] = p1[q, core, to, second] + cr[q, to, second]
            else:
                p1[q, core, to] = p1[q, core, to] + cr[q, to] + zr[q, way, step - 2]
            send((q, "r", way, step), p1.at[q, core, to], zr.at[q, way, step - 1], device)

    def scatter_y(q):
        arrived(q, "r", 0, 4)
        arrived(q, "r", 1, 4)
        yb[q] = p1[q, core, z] + cr[q, z] + (zr[q, 0, 3] + zr[q, 1, 3])
        send((q, "y"), yb.at[q], yr.at[q], y_far)

    def pass_on(q, k, part=slice(None)):
        piece = y1.at[q, core, at_z(k)] if part == slice(None) else y1.at[q, core, at_z(k), pl.ds(part, 8)]
        return piece

    def spread_0(q):
        arrived(q, "y")
        y1[q, core, z] = (yb[q] + yr[q]) * (1.0 / HALF_WIDTH)
        piece = pass_on(q, 0)
        send((q, "g", 0, 1), piece, piece, z_up)
        send((q, "g", 1, 1), piece, piece, z_down)
        send((q, "d", 0), piece, piece, sibling)

    def spread(step, q):
        for way, device in ((0, z_up), (1, z_down)):
            arrived(q, "g", way, step - 1)
            k = 9 - step if way == 0 else step - 1
            piece = pass_on(q, k) if step < 4 else pass_on(q, k, 8 * way)
            send((q, "g", way, step), piece, piece, device)
            piece = pass_on(q, k)
            send((q, "d", k), piece, piece, sibling)

    def spread_last(q):
        arrived(q, "g", 0, 4)
        arrived(q, "g", 1, 4)
        piece = pass_on(q, 4)
        send((q, "d", 4), piece, piece, sibling)

    def product_2(q):
        for k in range(8):
            arrived(q, "d", k)
        for half in range(2):
            high, low = split(y1[q, half].reshape(WIDE, HALF))
            cat1[0:WIDE, pl.ds(half * HALF, HALF)] = high
            cat1[WIDE:, pl.ds(half * HALF, HALF)] = low

        def step(i, carry):
            at = pl.multiple_of(i * 384, 128)
            over = (((1,), (1,)), ((), ()))
            both = lax.dot_general(h_hi[pl.ds(at, 384), :], cat1[...], over, preferred_element_type=F32)
            rest = lax.dot_general(h_lo[pl.ds(at, 384), :], cat1[0:WIDE, :], over, preferred_element_type=F32)
            p2[q, i] = (both[:, :WIDE] + (both[:, WIDE:] + rest)).reshape(4, OWN, WIDE)
            return carry

        lax.fori_loop(0, 2, step, 0)
        send((q, "s", 0, 1), p2.at[q, 0, at_x(2)], xr.at[q, 0, 0], x_up)
        send((q, "s", 1, 1), p2.at[q, 1, at_x(2)], xr.at[q, 1, 0], x_down)

    def reduce_1(q):
        for way, device in ((0, x_up), (1, x_down)):
            to = at_x(1) if way == 0 else at_x(3)
            arrived(q, "s", way, 1)
            xb[q, way, way] = p2[q, way, to] + xr[q, way, 0]
            xb[q, way, 1 - way] = p2[q, 1 - way, to]
            send((q, "s", way, 2), xb.at[q, way], xr.at[q, way, pl.ds(1, 2)], device)

    def reduce_2(q):
        arrived(q, "s", 0, 2)
        arrived(q, "s", 1, 2)
        for half in range(2):
            p2[q, half, x] = p2[q, half, x] + (xr[q, 0, 1 + half] + xr[q, 1, 1 + half])
        send((q, "l"), p2.at[q, 1 - y_lo, x], lr.at[q], y_near)

    def reduce_3(q):
        arrived(q, "l")
        o_ref[:, lanes(q)] = (2.0 / HALF_WIDTH) * (p2[q, y_lo, x] + lr[q]) - v_ref[:, lanes(q)]

    def split_matrix():
        offset = row * ROWS - col * COLS
        apart = lax.broadcasted_iota(jnp.int32, (16, COLS), 1) - lax.broadcasted_iota(jnp.int32, (16, COLS), 0)

        for i in range(PIECES):
            loads[i].wait()

            def step(j, carry):
                at = pl.multiple_of(i * OWN + j * 16, 16)
                inside = pl.multiple_of(j * 16, 16)
                value = h_in[i, pl.ds(inside, 16), :]
                high, low = split(value - jnp.where(apart == offset + at, F32(CENTER), F32(0.0)))
                h_hi[pl.ds(at, 16), :] = high
                h_lo[pl.ds(at, 16), :] = low
                return carry

            lax.fori_loop(0, OWN // 16, step, 0)

    stages = [
        gather_0, gather_1, gather_2, product_1, scatter_0,
        functools.partial(scatter, 2), functools.partial(scatter, 3), functools.partial(scatter, 4), scatter_y,
        spread_0, functools.partial(spread, 2), functools.partial(spread, 3), functools.partial(spread, 4), spread_last,
        product_2, reduce_1, reduce_2, reduce_3,
    ]
    plan = sorted((READY[s] + APART * q, q, s) for q in range(CHUNKS) for s in range(len(stages)))
    for q in range(CHUNKS):
        gather_0(q)
    split_pending = True
    for _, q, s in plan:
        if s == 0:
            continue
        if s == 3 and split_pending:
            split_matrix()
            split_pending = False
        stages[s](q)
    for copy in started.values():
        copy.wait_send()


def on_device(hamiltonian, vectors):
    n = CHUNKS
    copies = n * 38
    return pl.pallas_call(
        kernel,
        out_shape=jax.ShapeDtypeStruct((OWN, n * WIDE), F32),
        in_specs=[pl.BlockSpec(memory_space=pl.ANY), pl.BlockSpec(memory_space=pltpu.VMEM)],
        out_specs=pl.BlockSpec(memory_space=pltpu.VMEM),
        scratch_shapes=[
            pltpu.VMEM((PIECES, OWN, COLS), F32),
            pltpu.VMEM((ROWS, COLS), BF16),
            pltpu.VMEM((ROWS, COLS), BF16),
            pltpu.VMEM((n, 8, OWN, WIDE), F32),
            pltpu.VMEM((2 * WIDE, ROWS), BF16),
            pltpu.VMEM((n, 2, 8, 16, HALF), F32),
            pltpu.VMEM((n, 8, 16, HALF), F32),
            pltpu.VMEM((n, 2, 4, 16, HALF), F32),
            pltpu.VMEM((n, 16, HALF), F32),
            pltpu.VMEM((n, 16, HALF), F32),
            pltpu.VMEM((n, 2, 8, 16, HALF), F32),
            pltpu.VMEM((2 * WIDE, COLS), BF16),
            pltpu.VMEM((n, 2, 4, OWN, WIDE), F32),
            pltpu.VMEM((n, 2, 3, OWN, WIDE), F32),
            pltpu.VMEM((n, 2, 2, OWN, WIDE), F32),
            pltpu.VMEM((n, OWN, WIDE), F32),
            pltpu.SemaphoreType.DMA((PIECES,)),
            pltpu.SemaphoreType.DMA((copies,)),
            pltpu.SemaphoreType.DMA((copies,)),
        ],
        compiler_params=pltpu.CompilerParams(
            collective_id=0, has_side_effects=True, vmem_limit_bytes=64_000_000
        ),
    )(hamiltonian, vectors)


def solution(mesh):
    return jax.shard_map(
        on_device,
        mesh=mesh,
        in_specs=(P("row", "col"), P(("row", "col"), None)),
        out_specs=P(("row", "col"), None),
        check_vma=False,
    )
```

```python
import functools

import jax
import jax.numpy as jnp
from jax import lax
from jax.experimental import pallas as pl
from jax.experimental.pallas import tpu as pltpu
from jax.sharding import PartitionSpec as P

MESH = pl.DeviceIdType.MESH
F32 = jnp.float32
BF16 = jnp.bfloat16

CENTER = 0.6
HALF_WIDTH = 1.8

CHUNKS = 4
WIDE = 128
ROWS, COLS = 768, 3072
HALF = COLS // 2
STREAMS = 2
LANES = HALF // STREAMS
OWN = 96
PIECES = 8

MODES = ("zy", "yz", "zy", "yz")

HOP = {
    "z_up": 3.0, "z_down": 3.0, "x_up": 3.0, "x_down": 3.0, "x_far": 3.6, "y_near": 2.4, "y_far": 3.4, "sibling": 0.9,
    "xy_up": 3.7, "xy_down": 3.7, "xy_far": 4.3,
}
LINES = {
    "x_far": ("x_up", "x_down"), "y_near": ("y",), "y_far": ("y",),
    "xy_up": ("x_up", "y"), "xy_down": ("x_down", "y"), "xy_far": ("x_up", "x_down", "y"),
}
RATE = {"sibling": 500e3}
LINK_RATE = 46.5e3
BEGIN = 7.0
SPLIT, TURN, PRODUCT_1, PRODUCT_2, CONVERT = 0.8, 0.4, 2.1, 2.3, 0.4


def split(value):
    high = value.astype(BF16)
    return high, (value - high.astype(F32)).astype(BF16)


def ordered(tasks):
    now, free, landed, done, names = BEGIN, {}, {}, {}, []
    left = dict(tasks)
    while left:
        best, soonest = None, None
        for name, (rank, needs, _, _, _) in left.items():
            times = [landed.get(need[1:]) if need[0] == "m" else done.get(need) for need in needs]
            if None in times:
                continue
            at = max(times, default=0.0)
            if at > now:
                soonest = at if soonest is None else min(soonest, at)
            elif best is None or rank < best[0]:
                best = (rank, name)
        if best is None:
            now = soonest
            continue
        name = best[1]
        _, _, cost, messages, _ = left.pop(name)
        now += cost
        done[name] = now
        names.append(name)
        for key, link, size, _ in messages:
            lines = LINES.get(link, (link,))
            end = max([now] + [free.get(line, 0.0) for line in lines]) + size / RATE.get(link, LINK_RATE)
            free.update((line, end) for line in lines)
            landed[key] = end + HOP[link]
    return names


def kernel(h_ref, v_ref, o_ref, h_in, h_hi, h_lo, y0, cat0, p1, cr, fr, zr, yb, yr, y1, cat1, p2, xr, lr,
           h_sem, send_sem, recv_sem):
    row, col = lax.axis_index("row"), lax.axis_index("col")
    core, z, y_hi = lax.rem(row, 2), lax.rem(row // 2, 8), row // 16
    x, y_lo = lax.rem(col, 4), col // 4

    def at_z(k):
        return lax.rem(z + k, 8)

    def at_x(k):
        return lax.rem(x + k, 4)

    device = {
        "z_up": (y_hi * 16 + at_z(1) * 2 + core, col),
        "z_down": (y_hi * 16 + at_z(7) * 2 + core, col),
        "sibling": (row + 1 - 2 * core, col),
        "y_far": (lax.rem(row + 16, 32), col),
        "x_up": (row, y_lo * 4 + at_x(1)),
        "x_down": (row, y_lo * 4 + at_x(3)),
        "x_far": (row, y_lo * 4 + at_x(2)),
        "y_near": (row, lax.rem(col + 4, 8)),
        "xy_up": (row, (1 - y_lo) * 4 + at_x(1)),
        "xy_down": (row, (1 - y_lo) * 4 + at_x(3)),
        "xy_far": (row, (1 - y_lo) * 4 + at_x(2)),
    }
    around_z = ("z_up", "z_down")
    along_x = ("x_up", "x_down", "x_far")
    across = ("y_near", "xy_up", "xy_down", "xy_far")
    x_of = {"x_up": 1, "x_down": 3, "x_far": 2, "y_near": 0, "xy_up": 1, "xy_down": 3, "xy_far": 2}

    loads = [
        pltpu.make_async_copy(h_ref.at[pl.ds(OWN * i, OWN), :], h_in.at[i], h_sem.at[i]) for i in range(PIECES)
    ]
    for load in loads:
        load.start()

    barrier = pltpu.get_barrier_semaphore()
    for partner in device.values():
        pl.semaphore_signal(barrier, inc=1, device_id=partner, device_id_type=MESH)
    pl.semaphore_wait(barrier, len(device))

    tasks = {}

    def add(name, needs, cost, body=None, messages=(), rank=0):
        tasks[name] = ((rank, name[1]), needs, cost, messages, body)

    def lanes(q):
        return pl.ds(WIDE * q, WIDE)

    offset = row * ROWS - col * COLS
    apart = lax.broadcasted_iota(jnp.int32, (16, COLS), 1) - lax.broadcasted_iota(jnp.int32, (16, COLS), 0)

    def split_piece(i):
        loads[i].wait()

        def step(j, carry):
            at = pl.multiple_of(i * OWN + j * 16, 16)
            value = h_in[i, pl.ds(pl.multiple_of(j * 16, 16), 16), :]
            high, low = split(value - jnp.where(apart == offset + at, F32(CENTER), F32(0.0)))
            h_hi[pl.ds(at, 16), :] = high
            h_lo[pl.ds(at, 16), :] = low
            return carry

        lax.fori_loop(0, OWN // 16, step, 0)

    for i in range(PIECES):
        add(("split", i), [], SPLIT, functools.partial(split_piece, i), rank=9)
    all_split = [("split", i) for i in range(PIECES)]

    def chunk(q):
        def msg(*key):
            return ("m", q, *key)

        size = OWN * WIDE * 4

        def own():
            return v_ref.at[:, lanes(q)], y0.at[q, col]

        def other():
            ref = y0.at[q, lax.rem(col + 4, 8)]
            return ref, ref

        def keep_own():
            y0[q, col] = v_ref[:, lanes(q)]

        before = [("A1", q - 1) if q > 1 else ("A0", 0)] if q else []
        if q == 0:
            add(("A0", q), before, 0.1, keep_own, [((q, "a", link), link, size, own) for link in along_x + across])
            gathered = [msg("a", link) for link in along_x + across]
        else:
            add(("A0", q), before, 0.1, keep_own, [((q, "a", link), link, size, own) for link in ("y_near",) + along_x])
            add(("A1", q), [msg("a", "y_near")], 0.02, None,
                [((q, "b", link), link, size, other) for link in along_x])
            gathered = [msg(kind, link) for kind in "ab" for link in along_x]

        def turn():
            high, low = split(y0[q].reshape(ROWS, WIDE).T)
            cat0[0:WIDE, :] = high
            cat0[WIDE:, :] = low

        add(("T", q), gathered + all_split + ([("M1", q - 1, 1, STREAMS - 1)] if q else []),
            TURN, turn, rank=2)

        def product_1(h, u):
            half = core if h else 1 - core

            at = pl.ds(pl.multiple_of(half * HALF + u * LANES, 128), LANES)
            both = jnp.dot(cat0[...], h_hi[:, at], preferred_element_type=F32)
            rest = jnp.dot(cat0[0:WIDE, :], h_lo[:, at], preferred_element_type=F32)
            p1[q, half, u] = (both[:WIDE] + (both[WIDE:] + rest)).reshape(8, 2, 8, LANES)

        last = ("T", q)
        for h in range(2):
            for u in range(STREAMS):
                over = []
                if h == 0:
                    refs = functools.partial(lambda u: (p1.at[q, 1 - core, u], cr.at[q, u]), u)
                    over = [((q, "c", u), "sibling", WIDE * LANES * 4, refs)]
                add(("M1", q, h, u), [last], PRODUCT_1 / 2 / STREAMS, functools.partial(product_1, h, u), over, rank=2)
                last = ("M1", q, h, u)

        blocks = {}
        for u in range(STREAMS):
            blocks[0, u], blocks[1, u] = stream(q, u, msg)

        begun = []

        def product_2(h, u):
            half = 1 - core if h else core
            high, low = split(y1[q, half, u].reshape(WIDE, LANES))
            cat1[0:WIDE, :] = high
            cat1[WIDE:, :] = low
            columns = pl.ds(pl.multiple_of(half * HALF + u * LANES, 128), LANES)
            first = not begun
            begun.append(u)

            over = (((1,), (1,)), ((), ()))
            both = lax.dot_general(h_hi[:, columns], cat1[...], over, preferred_element_type=F32)
            rest = lax.dot_general(h_lo[:, columns], cat1[0:WIDE, :], over, preferred_element_type=F32)
            value = (both[:, :WIDE] + (both[:, WIDE:] + rest)).reshape(2, 4, OWN, WIDE)
            p2[q] = value if first else p2[q] + value

        for (h, u), needs in blocks.items():
            add(("M2", q, h, u), needs + all_split, (CONVERT + PRODUCT_2) / 2 / STREAMS,
                functools.partial(product_2, h, u), rank=1)

        products = [("M2", q, *at) for at in blocks]

        def apart_of(link, index):
            half = 1 - y_lo if link in across else y_lo
            return p2.at[q, half, at_x(x_of[link])], lr.at[q, index]

        def both_of(link, index):
            return p2.at[q, :, at_x(x_of[link])], xr.at[q, index]

        if q == CHUNKS - 1:
            links = along_x + across
            add(("S1", q), products, 0.05, None, [
                ((q, "s", link), link, size, functools.partial(apart_of, link, i)) for i, link in enumerate(links)
            ])

            def finish():
                value = p2[q, y_lo, x]
                for i in range(len(links)):
                    value = value + lr[q, i]
                o_ref[:, lanes(q)] = (2.0 / HALF_WIDTH) * value - v_ref[:, lanes(q)]

            add(("S4", q), [msg("s", link) for link in links], 0.1, finish)
            return

        add(("S1", q), products, 0.05, None, [
            ((q, "s", link), link, 2 * size, functools.partial(both_of, link, i)) for i, link in enumerate(along_x)
        ])

        def reduce_x():
            for half in range(2):
                p2[q, half, x] = (p2[q, half, x] + xr[q, 0, half]) + (xr[q, 1, half] + xr[q, 2, half])

        def reduce_y():
            o_ref[:, lanes(q)] = (2.0 / HALF_WIDTH) * (p2[q, y_lo, x] + lr[q, 0]) - v_ref[:, lanes(q)]

        add(("S3", q), [msg("s", link) for link in along_x], 0.1, reduce_x,
            [((q, "l"), "y_near", size, lambda: (p2.at[q, 1 - y_lo, x], lr.at[q, 0]))])
        add(("S4", q), [msg("l")], 0.06, reduce_y)

    count = {"z": 0, "y": 0}

    def stream(q, u, msg):
        mode = MODES[q][u]
        far = count[mode] % 2
        count[mode] += 1
        sheet = 8 * LANES * 4
        size = 2 * sheet if mode == "z" else sheet

        def part(ref, k):
            return ref.at[q, core, u, at_z(k)] if mode == "z" else ref.at[q, core, u, at_z(k), y_hi]

        def slot(way, step):
            return zr.at[q, u, way, step - 1] if mode == "z" else zr.at[q, u, way, step - 1, 0]

        def local(k):
            if mode == "z":
                return p1[q, core, u, at_z(k)] + cr[q, u, at_z(k)]
            return p1[q, core, u, at_z(k), y_hi] + cr[q, u, at_z(k), y_hi] + fr[q, u, at_z(k)]

        needs = [msg("c", u), ("M1", q, 1, u)]
        if mode == "y":
            def give():
                p1[q, core, u, :, 1 - y_hi] = p1[q, core, u, :, 1 - y_hi] + cr[q, u, :, 1 - y_hi]

            add(("Y", q, u), needs, 0.3, give,
                [((q, "f", u), "y_far", 8 * sheet, lambda: (p1.at[q, core, u, :, 1 - y_hi], fr.at[q, u]))])
            needs = [msg("f", u)]

        def ring(way, step):
            k = 5 - step if way == 0 else 3 + step
            value = local(k)
            if step > 2 or (step == 2 and way == far):
                value = value + slot(way, step - 1)[...]
            part(p1, k)[...] = value

        def to_ring(way, step):
            k = 5 - step if way == 0 else 3 + step
            return ((q, "r", u, way, step), around_z[way], size, lambda: (part(p1, k), slot(way, step)))

        add(("R", q, u, far, 1), needs, 0.12, functools.partial(ring, far, 1), [to_ring(far, 1)])
        for way in range(2):
            for step in (2, 3, 4):
                before = needs if step == 2 and way != far else [msg("r", u, way, step - 1)]
                add(("R", q, u, way, step), before, 0.1, functools.partial(ring, way, step), [to_ring(way, step)])

        def total():
            return local(0) + (slot(0, 4)[...] + slot(1, 4)[...])

        needs = [msg("r", u, 0, 4), msg("r", u, 1, 4)]
        if mode == "z":
            def meet():
                yb[q, u] = total()

            add(("RY", q, u), needs, 0.1, meet, [((q, "y", u), "y_far", size, lambda: (yb.at[q, u], yr.at[q, u]))])
            needs = [msg("y", u)]

        def settle():
            value = yb[q, u] + yr[q, u] if mode == "z" else total()
            part(y1, 0)[...] = value * (1.0 / HALF_WIDTH)

        def whole(k):
            return y1.at[q, core, u, at_z(k)]

        def twice(make, k):
            def refs():
                ref = make(k)
                return ref, ref

            return refs

        on = functools.partial(part, y1)

        def also(k):
            if mode == "z":
                return [((q, "d", u, k), "sibling", size, twice(whole, k))]
            return [((q, "v", u, k), "y_far", size, twice(on, k))]

        def onward(way, step, k):
            return ((q, "g", u, way, step), around_z[way], size, twice(on, k))

        add(("G", q, u), needs, 0.1, settle, [onward(0, 1, 0), onward(1, 1, 0)] + also(0))
        holder = {0: ("G", q, u)}
        for way in range(2):
            for step in (1, 2, 3, 4):
                if step == 4 and way != far:
                    continue
                k = (8 - step) % 8 if way == 0 else step
                further = [onward(way, step + 1, k)] if step < 3 or (step == 3 and way == far) else []
                add(("F", q, u, way, step), [msg("g", u, way, step)], 0.03, None, further + also(k))
                holder[k] = ("F", q, u, way, step)
        if mode == "y":
            for k in range(8):
                add(("V", q, u, k), [msg("v", u, k), holder[k]], 0.02, None,
                    [((q, "d", u, k), "sibling", 2 * size, twice(whole, k))])
                holder[k] = ("V", q, u, k)
        return list(holder.values()), [msg("d", u, k) for k in range(8)]

    for q in range(CHUNKS):
        chunk(q)

    copies, waited = {}, set()
    for name in ordered(tasks):
        _, needs, _, messages, body = tasks[name]
        for need in needs:
            if need[0] == "m" and need not in waited:
                waited.add(need)
                copies[need[1:]].wait_recv()
        if body is not None:
            body()
        for key, link, _, refs in messages:
            src, dst = refs()
            copy = pltpu.make_async_remote_copy(
                src_ref=src, dst_ref=dst, send_sem=send_sem.at[len(copies)], recv_sem=recv_sem.at[len(copies)],
                device_id=device[link], device_id_type=MESH,
            )
            copy.start()
            copies[key] = copy
    for copy in copies.values():
        copy.wait_send()


def on_device(hamiltonian, vectors):
    n = CHUNKS
    modes = "".join(MODES)
    copies = n * (7 + STREAMS + 4) + 3 + 23 * modes.count("z") + 31 * modes.count("y")
    return pl.pallas_call(
        kernel,
        out_shape=jax.ShapeDtypeStruct((OWN, n * WIDE), F32),
        in_specs=[pl.BlockSpec(memory_space=pl.ANY), pl.BlockSpec(memory_space=pltpu.VMEM)],
        out_specs=pl.BlockSpec(memory_space=pltpu.VMEM),
        scratch_shapes=[
            pltpu.VMEM((PIECES, OWN, COLS), F32),
            pltpu.VMEM((ROWS, COLS), BF16),
            pltpu.VMEM((ROWS, COLS), BF16),
            pltpu.VMEM((n, 8, OWN, WIDE), F32),
            pltpu.VMEM((2 * WIDE, ROWS), BF16),
            pltpu.VMEM((n, 2, STREAMS, 8, 2, 8, LANES), F32),
            pltpu.VMEM((n, STREAMS, 8, 2, 8, LANES), F32),
            pltpu.VMEM((n, STREAMS, 8, 8, LANES), F32),
            pltpu.VMEM((n, STREAMS, 2, 4, 2, 8, LANES), F32),
            pltpu.VMEM((n, STREAMS, 2, 8, LANES), F32),
            pltpu.VMEM((n, STREAMS, 2, 8, LANES), F32),
            pltpu.VMEM((n, 2, STREAMS, 8, 2, 8, LANES), F32),
            pltpu.VMEM((2 * WIDE, LANES), BF16),
            pltpu.VMEM((n, 2, 4, OWN, WIDE), F32),
            pltpu.VMEM((n, 3, 2, OWN, WIDE), F32),
            pltpu.VMEM((n, 7, OWN, WIDE), F32),
            pltpu.SemaphoreType.DMA((PIECES,)),
            pltpu.SemaphoreType.DMA((copies,)),
            pltpu.SemaphoreType.DMA((copies,)),
        ],
        compiler_params=pltpu.CompilerParams(
            collective_id=0, has_side_effects=True, vmem_limit_bytes=64_000_000
        ),
    )(hamiltonian, vectors)


def solution(mesh):
    return jax.shard_map(
        on_device,
        mesh=mesh,
        in_specs=(P("row", "col"), P(("row", "col"), None)),
        out_specs=P(("row", "col"), None),
        check_vma=False,
    )
```

```python
import functools

import jax
import jax.numpy as jnp
from jax import lax
from jax.experimental import pallas as pl
from jax.experimental.pallas import tpu as pltpu
from jax.sharding import PartitionSpec as P

MESH = pl.DeviceIdType.MESH
F32 = jnp.float32
BF16 = jnp.bfloat16

CENTER = 0.6
HALF_WIDTH = 1.8

CHUNKS = 4
WIDE = 128
ROWS, COLS = 768, 3072
HALF = COLS // 2
STREAMS = 2
LANES = HALF // STREAMS
OWN = 96
PIECES = 8

MODES = ("yz", "yz", "yz", "yz")
GATHER = "dyyy"
SUMS = "xxxd"

ORDER = (
    8, 4, 7, 2, 1, 5, 6, 62, 0, 3, 63, 116, 10, 11, 12, 13, 117, 170, 15, 14, 39, 43, 64, 65,
    66, 67, 68, 171, 69, 44, 40, 94, 93, 118, 119, 120, 121, 122, 16, 123, 20, 147, 151, 41, 45, 172, 97, 95,
    173, 174, 17, 70, 71, 175, 21, 148, 177, 152, 176, 201, 202, 42, 18, 74, 98, 128, 124, 72, 9, 153, 149, 22,
    96, 46, 75, 205, 19, 125, 178, 179, 129, 99, 203, 73, 76, 23, 126, 150, 47, 182, 180, 206, 100, 130, 77, 127,
    28, 24, 52, 154, 204, 183, 207, 48, 181, 81, 29, 131, 25, 78, 101, 184, 155, 208, 53, 49, 30, 82, 26, 132,
    32, 136, 185, 79, 105, 38, 156, 209, 33, 27, 83, 133, 50, 160, 54, 31, 189, 87, 102, 37, 86, 140, 106, 91,
    193, 137, 213, 146, 157, 80, 36, 35, 84, 134, 34, 55, 186, 51, 194, 190, 56, 103, 210, 107, 57, 58, 59, 85,
    88, 158, 161, 90, 92, 135, 214, 89, 109, 144, 187, 191, 110, 200, 104, 138, 108, 111, 112, 141, 211, 113, 188, 139,
    143, 215, 162, 192, 145, 195, 159, 165, 199, 196, 142, 163, 166, 164, 167, 216, 212, 197, 60, 219, 198, 220, 217, 218,
    114, 221, 61, 168, 115, 169, 222,
)

HOP = {
    "z_up": 3.0, "z_down": 3.0, "x_up": 3.0, "x_down": 3.0, "x_far": 3.6, "y_near": 2.4, "y_far": 3.4, "sibling": 0.9,
    "xy_up": 3.7, "xy_down": 3.7, "xy_far": 4.3,
}
LINES = {
    "x_far": ("x_up", "x_down"), "y_near": ("y",), "y_far": ("y",),
    "xy_up": ("x_up", "y"), "xy_down": ("x_down", "y"), "xy_far": ("x_up", "x_down", "y"),
}
RATE = {"sibling": 500e3}
LINK_RATE = 46.5e3
BEGIN = 7.0
SPLIT, TURN, PRODUCT_1, PRODUCT_2, CONVERT = 0.8, 0.4, 2.1, 2.3, 0.4


def split(value):
    high = value.astype(BF16)
    return high, (value - high.astype(F32)).astype(BF16)


def ordered(tasks):
    now, free, landed, done, names = BEGIN, {}, {}, {}, []
    left = dict(tasks)
    while left:
        best, soonest = None, None
        for name, (rank, needs, _, _, _) in left.items():
            times = [landed.get(need[1:]) if need[0] == "m" else done.get(need) for need in needs]
            if None in times:
                continue
            at = max(times, default=0.0)
            if at > now:
                soonest = at if soonest is None else min(soonest, at)
            elif best is None or rank < best[0]:
                best = (rank, name)
        if best is None:
            now = soonest
            continue
        name = best[1]
        _, _, cost, messages, _ = left.pop(name)
        now += cost
        done[name] = now
        names.append(name)
        for key, link, size, _ in messages:
            lines = LINES.get(link, (link,))
            end = max([now] + [free.get(line, 0.0) for line in lines]) + size / RATE.get(link, LINK_RATE)
            free.update((line, end) for line in lines)
            landed[key] = end + HOP[link]
    return names


def kernel(h_ref, v_ref, o_ref, v_in, out, h_in, h_hi, h_lo, y0, cat0, p1, cr, fr, zr, yb, yr, y1, cat1, p2, xr, lr, nr,
           v_sem, o_sem, h_sem, send_sem, recv_sem):
    row, col = lax.axis_index("row"), lax.axis_index("col")
    core, z, y_hi = lax.rem(row, 2), lax.rem(row // 2, 8), row // 16
    x, y_lo = lax.rem(col, 4), col // 4

    def at_z(k):
        return lax.rem(z + k, 8)

    def at_x(k):
        return lax.rem(x + k, 4)

    device = {
        "z_up": (y_hi * 16 + at_z(1) * 2 + core, col),
        "z_down": (y_hi * 16 + at_z(7) * 2 + core, col),
        "sibling": (row + 1 - 2 * core, col),
        "y_far": (lax.rem(row + 16, 32), col),
        "x_up": (row, y_lo * 4 + at_x(1)),
        "x_down": (row, y_lo * 4 + at_x(3)),
        "x_far": (row, y_lo * 4 + at_x(2)),
        "y_near": (row, lax.rem(col + 4, 8)),
        "xy_up": (row, (1 - y_lo) * 4 + at_x(1)),
        "xy_down": (row, (1 - y_lo) * 4 + at_x(3)),
        "xy_far": (row, (1 - y_lo) * 4 + at_x(2)),
    }
    around_z = ("z_up", "z_down")
    along_x = ("x_up", "x_down", "x_far")
    across = ("y_near", "xy_up", "xy_down", "xy_far")
    x_of = {"x_up": 1, "x_down": 3, "x_far": 2, "y_near": 0, "xy_up": 1, "xy_down": 3, "xy_far": 2}

    v_load = pltpu.make_async_copy(v_ref, v_in, v_sem)
    v_load.start()
    loads = [
        pltpu.make_async_copy(h_ref.at[pl.ds(OWN * i, OWN), :], h_in.at[i], h_sem.at[i]) for i in range(PIECES)
    ]
    for load in loads:
        load.start()

    barrier = pltpu.get_barrier_semaphore()
    for partner in device.values():
        pl.semaphore_signal(barrier, inc=1, device_id=partner, device_id_type=MESH)
    pl.semaphore_wait(barrier, len(device))

    tasks = {}

    def add(name, needs, cost, body=None, messages=(), rank=0):
        tasks[name] = ((rank, name[1]), needs, cost, messages, body)

    def lanes(q):
        return pl.ds(WIDE * q, WIDE)

    offset = row * ROWS - col * COLS
    apart = lax.broadcasted_iota(jnp.int32, (16, COLS), 1) - lax.broadcasted_iota(jnp.int32, (16, COLS), 0)

    def split_piece(i):
        loads[i].wait()

        def step(j, carry):
            at = pl.multiple_of(i * OWN + j * 16, 16)
            value = h_in[i, pl.ds(pl.multiple_of(j * 16, 16), 16), :]
            high, low = split(value - jnp.where(apart == offset + at, F32(CENTER), F32(0.0)))
            h_hi[pl.ds(at, 16), :] = high
            h_lo[pl.ds(at, 16), :] = low
            return carry

        lax.fori_loop(0, OWN // 16, step, 0)

    for i in range(PIECES):
        add(("split", i), [], SPLIT, functools.partial(split_piece, i), rank=9)
    all_split = [("split", i) for i in range(PIECES)]

    def chunk(q):
        def msg(*key):
            return ("m", q, *key)

        size = OWN * WIDE * 4

        def own():
            return v_ref.at[:, lanes(q)], y0.at[q, col]

        def slice_of(half, k):
            ref = y0.at[q, (y_lo + half - 2 * half * y_lo) * 4 + at_x(k)]
            return ref, ref

        before = [("A0", 0)] if q == 1 else [("A1", q - 1)] if q else []
        if GATHER[q] == "d":
            add(("A0", q), before, 0.1, None, [((q, "a", link), link, size, own) for link in along_x + across])
            add(("A1", q), [("A0", q)], 0.0)
            gathered = [msg("a", link) for link in along_x + across]
        else:
            add(("A0", q), before, 0.1, None, [((q, "a", link), link, size, own) for link in ("y_near",) + along_x])
            if GATHER[q] == "y":
                add(("A1", q), [msg("a", "y_near")], 0.02, None,
                    [((q, "b", link), link, size, functools.partial(slice_of, 1, 0)) for link in along_x])
            else:
                for n, link in enumerate(along_x):
                    k = (4 - x_of[link]) % 4
                    add(("A%d" % (n + 1), q), [msg("a", link)], 0.02, None,
                        [((q, "b", link), "y_near", size, functools.partial(slice_of, 0, k))])
            gathered = [msg("a", link) for link in ("y_near",) + along_x] + [msg("b", link) for link in along_x]

        def turn():
            if not turned:
                v_load.wait()
            turned.append(q)
            y0[q, col] = v_in[:, lanes(q)]
            high, low = split(y0[q].reshape(ROWS, WIDE).T)
            cat0[0:WIDE, :] = high
            cat0[WIDE:, :] = low

        add(("T", q), gathered + all_split + ([("M1", q - 1, 1, STREAMS - 1)] if q else []),
            TURN, turn, rank=2)

        def product_1(h, u):
            half = core if h else 1 - core

            at = pl.ds(pl.multiple_of(half * HALF + u * LANES, 128), LANES)
            both = jnp.dot(cat0[...], h_hi[:, at], preferred_element_type=F32)
            rest = jnp.dot(cat0[0:WIDE, :], h_lo[:, at], preferred_element_type=F32)
            p1[q, half, u] = (both[:WIDE] + (both[WIDE:] + rest)).reshape(8, 2, 8, LANES)

        last = ("T", q)
        for h in range(2):
            for u in range(STREAMS):
                over = []
                if h == 0:
                    refs = functools.partial(lambda u: (p1.at[q, 1 - core, u], cr.at[q, u]), u)
                    over = [((q, "c", u), "sibling", WIDE * LANES * 4, refs)]
                add(("M1", q, h, u), [last], PRODUCT_1 / 2 / STREAMS, functools.partial(product_1, h, u), over, rank=2)
                last = ("M1", q, h, u)

        blocks = {}
        for u in range(STREAMS):
            blocks[0, u], blocks[1, u] = stream(q, u, msg)

        begun = []

        def product_2(h, u):
            half = 1 - core if h else core
            high, low = split(y1[q, half, u].reshape(WIDE, LANES))
            cat1[0:WIDE, :] = high
            cat1[WIDE:, :] = low
            columns = pl.ds(pl.multiple_of(half * HALF + u * LANES, 128), LANES)
            first = not begun
            begun.append(u)

            over = (((1,), (1,)), ((), ()))
            both = lax.dot_general(h_hi[:, columns], cat1[...], over, preferred_element_type=F32)
            rest = lax.dot_general(h_lo[:, columns], cat1[0:WIDE, :], over, preferred_element_type=F32)
            value = (both[:, :WIDE] + (both[:, WIDE:] + rest)).reshape(2, 4, OWN, WIDE)
            p2[q] = value if first else p2[q] + value

        for (h, u), needs in blocks.items():
            add(("M2", q, h, u), needs + all_split, (CONVERT + PRODUCT_2) / 2 / STREAMS,
                functools.partial(product_2, h, u), rank=1)

        products = [("M2", q, *at) for at in blocks]

        def apart_of(link, index):
            half = 1 - y_lo if link in across else y_lo
            return p2.at[q, half, at_x(x_of[link])], lr.at[q, index]

        def both_of(link, index):
            return p2.at[q, :, at_x(x_of[link])], xr.at[q, index]

        if SUMS[q] == "d":
            links = along_x + across
            add(("S1", q), products, 0.05, None, [
                ((q, "s", link), link, size, functools.partial(apart_of, link, i)) for i, link in enumerate(links)
            ])

            def finish():
                value = p2[q, y_lo, x]
                for i in range(len(links)):
                    value = value + lr[q, i]
                put(q, value)

            add(("S4", q), [msg("s", link) for link in links], 0.1, finish)
            return

        if SUMS[q] == "y":
            def reduce_near():
                p2[q, y_lo] = p2[q, y_lo] + nr[q]

            def near_of(link, index):
                return p2.at[q, y_lo, at_x(x_of[link])], lr.at[q, index]

            def finish_near():
                value = (p2[q, y_lo, x] + lr[q, 0]) + (lr[q, 1] + lr[q, 2])
                put(q, value)

            add(("S1", q), products, 0.05, None,
                [((q, "l"), "y_near", 4 * size, lambda: (p2.at[q, 1 - y_lo], nr.at[q]))])
            add(("S3", q), [msg("l")], 0.15, reduce_near,
                [((q, "s", link), link, size, functools.partial(near_of, link, i)) for i, link in enumerate(along_x)])
            add(("S4", q), [msg("s", link) for link in along_x], 0.1, finish_near)
            return

        add(("S1", q), products, 0.05, None, [
            ((q, "s", link), link, 2 * size, functools.partial(both_of, link, i)) for i, link in enumerate(along_x)
        ])

        def reduce_x():
            for half in range(2):
                p2[q, half, x] = (p2[q, half, x] + xr[q, 0, half]) + (xr[q, 1, half] + xr[q, 2, half])

        def reduce_y():
            put(q, p2[q, y_lo, x] + lr[q, 0])

        add(("S3", q), [msg("s", link) for link in along_x], 0.1, reduce_x,
            [((q, "l"), "y_near", size, lambda: (p2.at[q, 1 - y_lo, x], lr.at[q, 0]))])
        add(("S4", q), [msg("l")], 0.06, reduce_y)

    count, turned, stores = {"z": 0, "y": 0}, [], []

    def put(q, total):
        out[q] = (2.0 / HALF_WIDTH) * total - v_in[:, lanes(q)]
        store = pltpu.make_async_copy(out.at[q], o_ref.at[:, lanes(q)], o_sem.at[q])
        store.start()
        stores.append(store)

    def stream(q, u, msg):
        mode = MODES[q][u]
        far = count[mode] % 2
        count[mode] += 1
        sheet = 8 * LANES * 4
        size = 2 * sheet if mode == "z" else sheet

        def part(ref, k):
            return ref.at[q, core, u, at_z(k)] if mode == "z" else ref.at[q, core, u, at_z(k), y_hi]

        def slot(way, step):
            return zr.at[q, u, way, step - 1] if mode == "z" else zr.at[q, u, way, step - 1, 0]

        def local(k):
            if mode == "z":
                return p1[q, core, u, at_z(k)] + cr[q, u, at_z(k)]
            return p1[q, core, u, at_z(k), y_hi] + cr[q, u, at_z(k), y_hi] + fr[q, u, at_z(k)]

        needs = [msg("c", u), ("M1", q, 1, u)]
        if mode == "y":
            def give():
                p1[q, core, u, :, 1 - y_hi] = p1[q, core, u, :, 1 - y_hi] + cr[q, u, :, 1 - y_hi]

            add(("Y", q, u), needs, 0.3, give,
                [((q, "f", u), "y_far", 8 * sheet, lambda: (p1.at[q, core, u, :, 1 - y_hi], fr.at[q, u]))])
            needs = [msg("f", u)]

        def ring(way, step):
            k = 5 - step if way == 0 else 3 + step
            value = local(k)
            if step > 2 or (step == 2 and way == far):
                value = value + slot(way, step - 1)[...]
            part(p1, k)[...] = value

        def to_ring(way, step):
            k = 5 - step if way == 0 else 3 + step
            return ((q, "r", u, way, step), around_z[way], size, lambda: (part(p1, k), slot(way, step)))

        add(("R", q, u, far, 1), needs, 0.12, functools.partial(ring, far, 1), [to_ring(far, 1)])
        for way in range(2):
            for step in (2, 3, 4):
                before = needs if step == 2 and way != far else [msg("r", u, way, step - 1)]
                add(("R", q, u, way, step), before, 0.1, functools.partial(ring, way, step), [to_ring(way, step)])

        def total():
            return local(0) + (slot(0, 4)[...] + slot(1, 4)[...])

        needs = [msg("r", u, 0, 4), msg("r", u, 1, 4)]
        if mode == "z":
            def meet():
                yb[q, u] = total()

            add(("RY", q, u), needs, 0.1, meet, [((q, "y", u), "y_far", size, lambda: (yb.at[q, u], yr.at[q, u]))])
            needs = [msg("y", u)]

        def settle():
            value = yb[q, u] + yr[q, u] if mode == "z" else total()
            part(y1, 0)[...] = value * (1.0 / HALF_WIDTH)

        def whole(k):
            return y1.at[q, core, u, at_z(k)]

        def twice(make, k):
            def refs():
                ref = make(k)
                return ref, ref

            return refs

        on = functools.partial(part, y1)

        def also(k):
            if mode == "z":
                return [((q, "d", u, k), "sibling", size, twice(whole, k))]
            return [((q, "v", u, k), "y_far", size, twice(on, k))]

        def onward(way, step, k):
            return ((q, "g", u, way, step), around_z[way], size, twice(on, k))

        add(("G", q, u), needs, 0.1, settle, [onward(0, 1, 0), onward(1, 1, 0)] + also(0))
        holder = {0: ("G", q, u)}
        for way in range(2):
            for step in (1, 2, 3, 4):
                if step == 4 and way != far:
                    continue
                k = (8 - step) % 8 if way == 0 else step
                further = [onward(way, step + 1, k)] if step < 3 or (step == 3 and way == far) else []
                add(("F", q, u, way, step), [msg("g", u, way, step)], 0.03, None, further + also(k))
                holder[k] = ("F", q, u, way, step)
        if mode == "y":
            for k in range(8):
                add(("V", q, u, k), [msg("v", u, k), holder[k]], 0.02, None,
                    [((q, "d", u, k), "sibling", 2 * size, twice(whole, k))])
                holder[k] = ("V", q, u, k)
        return list(holder.values()), [msg("d", u, k) for k in range(8)]

    for q in range(CHUNKS):
        chunk(q)

    copies, waited = {}, set()
    every = list(tasks)
    for name in [every[i] for i in ORDER]:
        _, needs, _, messages, body = tasks[name]
        for need in needs:
            if need[0] == "m" and need not in waited:
                waited.add(need)
                copies[need[1:]].wait_recv()
        if body is not None:
            body()
        for key, link, _, refs in messages:
            src, dst = refs()
            copy = pltpu.make_async_remote_copy(
                src_ref=src, dst_ref=dst, send_sem=send_sem.at[len(copies)], recv_sem=recv_sem.at[len(copies)],
                device_id=device[link], device_id_type=MESH,
            )
            copy.start()
            copies[key] = copy
    for copy in copies.values():
        copy.wait_send()
    for store in stores:
        store.wait()


def on_device(hamiltonian, vectors):
    n = CHUNKS
    modes = "".join(MODES)
    copies = n * (7 + STREAMS + 4) + 3 * SUMS.count("d") + 23 * modes.count("z") + 31 * modes.count("y")
    return pl.pallas_call(
        kernel,
        out_shape=jax.ShapeDtypeStruct((OWN, n * WIDE), F32),
        in_specs=[pl.BlockSpec(memory_space=pl.ANY)] * 2,
        out_specs=pl.BlockSpec(memory_space=pl.ANY),
        scratch_shapes=[
            pltpu.VMEM((OWN, n * WIDE), F32),
            pltpu.VMEM((n, OWN, WIDE), F32),
            pltpu.VMEM((PIECES, OWN, COLS), F32),
            pltpu.VMEM((ROWS, COLS), BF16),
            pltpu.VMEM((ROWS, COLS), BF16),
            pltpu.VMEM((n, 8, OWN, WIDE), F32),
            pltpu.VMEM((2 * WIDE, ROWS), BF16),
            pltpu.VMEM((n, 2, STREAMS, 8, 2, 8, LANES), F32),
            pltpu.VMEM((n, STREAMS, 8, 2, 8, LANES), F32),
            pltpu.VMEM((n, STREAMS, 8, 8, LANES), F32),
            pltpu.VMEM((n, STREAMS, 2, 4, 2, 8, LANES), F32),
            pltpu.VMEM((n, STREAMS, 2, 8, LANES), F32),
            pltpu.VMEM((n, STREAMS, 2, 8, LANES), F32),
            pltpu.VMEM((n, 2, STREAMS, 8, 2, 8, LANES), F32),
            pltpu.VMEM((2 * WIDE, LANES), BF16),
            pltpu.VMEM((n, 2, 4, OWN, WIDE), F32),
            pltpu.VMEM((n, 3, 2, OWN, WIDE), F32),
            pltpu.VMEM((n, 7, OWN, WIDE), F32),
            pltpu.VMEM((n, 4, OWN, WIDE), F32),
            pltpu.SemaphoreType.DMA,
            pltpu.SemaphoreType.DMA((n,)),
            pltpu.SemaphoreType.DMA((PIECES,)),
            pltpu.SemaphoreType.DMA((copies,)),
            pltpu.SemaphoreType.DMA((copies,)),
        ],
        compiler_params=pltpu.CompilerParams(
            collective_id=0, has_side_effects=True, vmem_limit_bytes=66_000_000
        ),
    )(hamiltonian, vectors)


def solution(mesh):
    return jax.shard_map(
        on_device,
        mesh=mesh,
        in_specs=(P("row", "col"), P(("row", "col"), None)),
        out_specs=P(("row", "col"), None),
        check_vma=False,
    )
```

```python
import functools

import jax
import jax.numpy as jnp
from jax import lax
from jax.experimental import pallas as pl
from jax.experimental.pallas import tpu as pltpu
from jax.sharding import PartitionSpec as P

MESH = pl.DeviceIdType.MESH
F32 = jnp.float32
BF16 = jnp.bfloat16

CENTER = 0.6
HALF_WIDTH = 1.8

CHUNKS = 4
WIDE = 128
ROWS, COLS = 768, 3072
HALF = COLS // 2
STREAMS = 2
LANES = HALF // STREAMS
OWN = 96
PIECES = 8

MODES = ("zy", "yz", "zy", "yz")
GATHER = "dyyy"
SUMS = "xxxd"

ORDER = (
    8, 3, 5, 1, 9, 62, 2, 0, 6, 4, 7, 63, 116, 10, 11, 12, 13, 15, 14, 117, 170, 19, 31, 64,
    65, 66, 16, 67, 69, 171, 68, 20, 94, 93, 32, 118, 119, 120, 36, 121, 17, 127, 123, 122, 139, 70, 33, 21,
    95, 172, 173, 97, 174, 175, 71, 37, 18, 176, 177, 74, 140, 201, 34, 124, 144, 98, 202, 72, 38, 75, 141, 178,
    128, 35, 179, 205, 22, 125, 96, 145, 76, 73, 182, 203, 39, 99, 142, 180, 206, 126, 129, 77, 183, 23, 146, 40,
    204, 100, 207, 143, 181, 44, 78, 130, 184, 81, 24, 41, 28, 101, 147, 79, 208, 47, 45, 185, 25, 82, 131, 53,
    105, 42, 148, 54, 46, 29, 102, 80, 152, 83, 189, 26, 91, 132, 209, 43, 48, 149, 106, 136, 50, 30, 84, 186,
    103, 153, 27, 190, 86, 55, 213, 162, 87, 52, 133, 49, 51, 57, 107, 150, 56, 58, 85, 187, 137, 59, 92, 154,
    200, 191, 88, 90, 89, 155, 210, 104, 109, 214, 161, 193, 134, 157, 110, 151, 108, 156, 111, 112, 113, 188, 160, 192,
    138, 211, 215, 135, 158, 163, 159, 165, 164, 166, 195, 167, 212, 194, 199, 198, 196, 60, 197, 217, 216, 219, 220, 114,
    218, 221, 168, 61, 222, 115, 169,
)

HOP = {
    "z_up": 3.0, "z_down": 3.0, "x_up": 3.0, "x_down": 3.0, "x_far": 3.6, "y_near": 2.4, "y_far": 3.4, "sibling": 0.9,
    "xy_up": 3.7, "xy_down": 3.7, "xy_far": 4.3,
}
LINES = {
    "x_far": ("x_up", "x_down"), "y_near": ("y",), "y_far": ("y",),
    "xy_up": ("x_up", "y"), "xy_down": ("x_down", "y"), "xy_far": ("x_up", "x_down", "y"),
}
RATE = {"sibling": 500e3}
LINK_RATE = 46.5e3
BEGIN = 7.0
SPLIT, TURN, PRODUCT_1, PRODUCT_2, CONVERT = 0.8, 0.4, 2.1, 2.3, 0.4


def split(value):
    high = value.astype(BF16)
    return high, (value - high.astype(F32)).astype(BF16)


def ordered(tasks):
    now, free, landed, done, names = BEGIN, {}, {}, {}, []
    left = dict(tasks)
    while left:
        best, soonest = None, None
        for name, (rank, needs, _, _, _) in left.items():
            times = [landed.get(need[1:]) if need[0] == "m" else done.get(need) for need in needs]
            if None in times:
                continue
            at = max(times, default=0.0)
            if at > now:
                soonest = at if soonest is None else min(soonest, at)
            elif best is None or rank < best[0]:
                best = (rank, name)
        if best is None:
            now = soonest
            continue
        name = best[1]
        _, _, cost, messages, _ = left.pop(name)
        now += cost
        done[name] = now
        names.append(name)
        for key, link, size, _ in messages:
            lines = LINES.get(link, (link,))
            end = max([now] + [free.get(line, 0.0) for line in lines]) + size / RATE.get(link, LINK_RATE)
            free.update((line, end) for line in lines)
            landed[key] = end + HOP[link]
    return names


def kernel(h_ref, v_ref, o_ref, v_in, out, h_in, h_hi, h_lo, y0, cat0, p1, cr, fr, zr, yb, yr, y1, cat1, p2, xr, lr, nr,
           v_sem, o_sem, h_sem, send_sem, recv_sem):
    row, col = lax.axis_index("row"), lax.axis_index("col")
    core, z, y_hi = lax.rem(row, 2), lax.rem(row // 2, 8), row // 16
    x, y_lo = lax.rem(col, 4), col // 4

    def at_z(k):
        return lax.rem(z + k, 8)

    def at_x(k):
        return lax.rem(x + k, 4)

    device = {
        "z_up": (y_hi * 16 + at_z(1) * 2 + core, col),
        "z_down": (y_hi * 16 + at_z(7) * 2 + core, col),
        "sibling": (row + 1 - 2 * core, col),
        "y_far": (lax.rem(row + 16, 32), col),
        "x_up": (row, y_lo * 4 + at_x(1)),
        "x_down": (row, y_lo * 4 + at_x(3)),
        "x_far": (row, y_lo * 4 + at_x(2)),
        "y_near": (row, lax.rem(col + 4, 8)),
        "xy_up": (row, (1 - y_lo) * 4 + at_x(1)),
        "xy_down": (row, (1 - y_lo) * 4 + at_x(3)),
        "xy_far": (row, (1 - y_lo) * 4 + at_x(2)),
    }
    around_z = ("z_up", "z_down")
    along_x = ("x_far", "x_up", "x_down")
    across = ("xy_far", "xy_up", "xy_down", "y_near")
    straight = ("xy_far", "x_far", "xy_up", "xy_down", "x_up", "x_down", "y_near")
    x_of = {"x_up": 1, "x_down": 3, "x_far": 2, "y_near": 0, "xy_up": 1, "xy_down": 3, "xy_far": 2}

    v_load = pltpu.make_async_copy(v_ref, v_in, v_sem)
    v_load.start()
    loads = [
        pltpu.make_async_copy(h_ref.at[pl.ds(OWN * i, OWN), :], h_in.at[i], h_sem.at[i]) for i in range(PIECES)
    ]
    for load in loads:
        load.start()

    barrier = pltpu.get_barrier_semaphore()
    for partner in device.values():
        pl.semaphore_signal(barrier, inc=1, device_id=partner, device_id_type=MESH)
    pl.semaphore_wait(barrier, len(device))

    tasks = {}

    def add(name, needs, cost, body=None, messages=(), rank=0):
        tasks[name] = ((rank, name[1]), needs, cost, messages, body)

    def lanes(q):
        return pl.ds(WIDE * q, WIDE)

    offset = row * ROWS - col * COLS
    apart = lax.broadcasted_iota(jnp.int32, (16, COLS), 1) - lax.broadcasted_iota(jnp.int32, (16, COLS), 0)

    def split_piece(i):
        loads[i].wait()

        def step(j, carry):
            at = pl.multiple_of(i * OWN + j * 16, 16)
            value = h_in[i, pl.ds(pl.multiple_of(j * 16, 16), 16), :]
            high, low = split(value - jnp.where(apart == offset + at, F32(CENTER), F32(0.0)))
            h_hi[pl.ds(at, 16), :] = high
            h_lo[pl.ds(at, 16), :] = low
            return carry

        lax.fori_loop(0, OWN // 16, step, 0)

    for i in range(PIECES):
        add(("split", i), [], SPLIT, functools.partial(split_piece, i), rank=9)
    all_split = [("split", i) for i in range(PIECES)]

    def chunk(q):
        def msg(*key):
            return ("m", q, *key)

        size = OWN * WIDE * 4

        def own():
            return v_ref.at[:, lanes(q)], y0.at[q, col]

        def slice_of(half, k):
            ref = y0.at[q, (y_lo + half - 2 * half * y_lo) * 4 + at_x(k)]
            return ref, ref

        before = [("A0", 0)] if q == 1 else [("A1", q - 1)] if q else []
        if GATHER[q] == "d":
            add(("A0", q), before, 0.1, None, [((q, "a", link), link, size, own) for link in straight])
            add(("A1", q), [("A0", q)], 0.0)
            gathered = [msg("a", link) for link in straight]
        else:
            add(("A0", q), before, 0.1, None, [((q, "a", link), link, size, own) for link in ("y_near",) + along_x])
            if GATHER[q] == "y":
                add(("A1", q), [msg("a", "y_near")], 0.02, None,
                    [((q, "b", link), link, size, functools.partial(slice_of, 1, 0)) for link in along_x])
            else:
                for n, link in enumerate(along_x):
                    k = (4 - x_of[link]) % 4
                    add(("A%d" % (n + 1), q), [msg("a", link)], 0.02, None,
                        [((q, "b", link), "y_near", size, functools.partial(slice_of, 0, k))])
            gathered = [msg("a", link) for link in ("y_near",) + along_x] + [msg("b", link) for link in along_x]

        def turn():
            if not turned:
                v_load.wait()
            turned.append(q)
            y0[q, col] = v_in[:, lanes(q)]
            high, low = split(y0[q].reshape(ROWS, WIDE).T)
            cat0[0:WIDE, :] = high
            cat0[WIDE:, :] = low

        add(("T", q), gathered + all_split + ([("M1", q - 1, 1, STREAMS - 1)] if q else []),
            TURN, turn, rank=2)

        def product_1(h, u):
            half = core if h else 1 - core

            at = pl.ds(pl.multiple_of(half * HALF + u * LANES, 128), LANES)
            both = jnp.dot(cat0[...], h_hi[:, at], preferred_element_type=F32)
            rest = jnp.dot(cat0[0:WIDE, :], h_lo[:, at], preferred_element_type=F32)
            p1[q, half, u] = (both[:WIDE] + (both[WIDE:] + rest)).reshape(8, 2, 8, LANES)

        last = ("T", q)
        for h in range(2):
            for u in range(STREAMS):
                over = []
                if h == 0:
                    refs = functools.partial(lambda u: (p1.at[q, 1 - core, u], cr.at[q, u]), u)
                    over = [((q, "c", u), "sibling", WIDE * LANES * 4, refs)]
                add(("M1", q, h, u), [last], PRODUCT_1 / 2 / STREAMS, functools.partial(product_1, h, u), over, rank=2)
                last = ("M1", q, h, u)

        blocks = {}
        for u in range(STREAMS):
            blocks[0, u], blocks[1, u] = stream(q, u, msg)

        begun = []

        def product_2(h, u):
            half = 1 - core if h else core
            high, low = split(y1[q, half, u].reshape(WIDE, LANES))
            cat1[0:WIDE, :] = high
            cat1[WIDE:, :] = low
            columns = pl.ds(pl.multiple_of(half * HALF + u * LANES, 128), LANES)
            first = not begun
            begun.append(u)

            over = (((1,), (1,)), ((), ()))
            both = lax.dot_general(h_hi[:, columns], cat1[...], over, preferred_element_type=F32)
            rest = lax.dot_general(h_lo[:, columns], cat1[0:WIDE, :], over, preferred_element_type=F32)
            value = (both[:, :WIDE] + (both[:, WIDE:] + rest)).reshape(2, 4, OWN, WIDE)
            p2[q] = value if first else p2[q] + value

        for (h, u), needs in blocks.items():
            add(("M2", q, h, u), needs + all_split, (CONVERT + PRODUCT_2) / 2 / STREAMS,
                functools.partial(product_2, h, u), rank=1)

        products = [("M2", q, *at) for at in blocks]

        def apart_of(link, index):
            half = 1 - y_lo if link in across else y_lo
            return p2.at[q, half, at_x(x_of[link])], lr.at[q, index]

        def both_of(link, index):
            return p2.at[q, :, at_x(x_of[link])], xr.at[q, index]

        if SUMS[q] == "d":
            links = straight
            add(("S1", q), products, 0.05, None, [
                ((q, "s", link), link, size, functools.partial(apart_of, link, i)) for i, link in enumerate(links)
            ])

            def finish():
                value = p2[q, y_lo, x]
                for i in range(len(links)):
                    value = value + lr[q, i]
                put(q, value)

            add(("S4", q), [msg("s", link) for link in links], 0.1, finish)
            return

        if SUMS[q] == "y":
            def reduce_near():
                p2[q, y_lo] = p2[q, y_lo] + nr[q]

            def near_of(link, index):
                return p2.at[q, y_lo, at_x(x_of[link])], lr.at[q, index]

            def finish_near():
                value = (p2[q, y_lo, x] + lr[q, 0]) + (lr[q, 1] + lr[q, 2])
                put(q, value)

            add(("S1", q), products, 0.05, None,
                [((q, "l"), "y_near", 4 * size, lambda: (p2.at[q, 1 - y_lo], nr.at[q]))])
            add(("S3", q), [msg("l")], 0.15, reduce_near,
                [((q, "s", link), link, size, functools.partial(near_of, link, i)) for i, link in enumerate(along_x)])
            add(("S4", q), [msg("s", link) for link in along_x], 0.1, finish_near)
            return

        add(("S1", q), products, 0.05, None, [
            ((q, "s", link), link, 2 * size, functools.partial(both_of, link, i)) for i, link in enumerate(along_x)
        ])

        def reduce_x():
            for half in range(2):
                p2[q, half, x] = (p2[q, half, x] + xr[q, 0, half]) + (xr[q, 1, half] + xr[q, 2, half])

        def reduce_y():
            put(q, p2[q, y_lo, x] + lr[q, 0])

        add(("S3", q), [msg("s", link) for link in along_x], 0.1, reduce_x,
            [((q, "l"), "y_near", size, lambda: (p2.at[q, 1 - y_lo, x], lr.at[q, 0]))])
        add(("S4", q), [msg("l")], 0.06, reduce_y)

    count, turned, stores = {"z": 0, "y": 0}, [], []

    def put(q, total):
        out[q] = (2.0 / HALF_WIDTH) * total - v_in[:, lanes(q)]
        store = pltpu.make_async_copy(out.at[q], o_ref.at[:, lanes(q)], o_sem.at[q])
        store.start()
        stores.append(store)

    def stream(q, u, msg):
        mode = MODES[q][u]
        far = count[mode] % 2
        count[mode] += 1
        sheet = 8 * LANES * 4
        size = 2 * sheet if mode == "z" else sheet

        def part(ref, k):
            return ref.at[q, core, u, at_z(k)] if mode == "z" else ref.at[q, core, u, at_z(k), y_hi]

        def slot(way, step):
            return zr.at[q, u, way, step - 1] if mode == "z" else zr.at[q, u, way, step - 1, 0]

        def local(k):
            if mode == "z":
                return p1[q, core, u, at_z(k)] + cr[q, u, at_z(k)]
            return p1[q, core, u, at_z(k), y_hi] + cr[q, u, at_z(k), y_hi] + fr[q, u, at_z(k)]

        needs = [msg("c", u), ("M1", q, 1, u)]
        if mode == "y":
            def give():
                p1[q, core, u, :, 1 - y_hi] = p1[q, core, u, :, 1 - y_hi] + cr[q, u, :, 1 - y_hi]

            def across_y(k):
                return p1.at[q, core, u, at_z(k), 1 - y_hi], fr.at[q, u, at_z(k)]

            add(("Y", q, u), needs, 0.3, give,
                [((q, "f", u, k), "y_far", sheet, functools.partial(across_y, k)) for k in (4, 3, 5, 2, 6, 1, 7, 0)])

        def ring(way, step):
            k = 5 - step if way == 0 else 3 + step
            value = local(k)
            if step > 2 or (step == 2 and way == far):
                value = value + slot(way, step - 1)[...]
            part(p1, k)[...] = value

        def to_ring(way, step):
            k = 5 - step if way == 0 else 3 + step
            return ((q, "r", u, way, step), around_z[way], size, lambda: (part(p1, k), slot(way, step)))

        def ready(k):
            return [msg("f", u, k)] if mode == "y" else needs

        add(("R", q, u, far, 1), ready(4), 0.12, functools.partial(ring, far, 1), [to_ring(far, 1)])
        for way in range(2):
            for step in (2, 3, 4):
                before = ready(5 - step if way == 0 else 3 + step)
                if step > 2 or way == far:
                    before = before + [msg("r", u, way, step - 1)]
                add(("R", q, u, way, step), before, 0.1, functools.partial(ring, way, step), [to_ring(way, step)])

        def total():
            return local(0) + (slot(0, 4)[...] + slot(1, 4)[...])

        needs = ready(0) + [msg("r", u, 0, 4), msg("r", u, 1, 4)]
        if mode == "z":
            def meet():
                yb[q, u] = total()

            add(("RY", q, u), needs, 0.1, meet, [((q, "y", u), "y_far", size, lambda: (yb.at[q, u], yr.at[q, u]))])
            needs = [msg("y", u)]

        def settle():
            value = yb[q, u] + yr[q, u] if mode == "z" else total()
            part(y1, 0)[...] = value * (1.0 / HALF_WIDTH)

        def whole(k):
            return y1.at[q, core, u, at_z(k)]

        def twice(make, k):
            def refs():
                ref = make(k)
                return ref, ref

            return refs

        on = functools.partial(part, y1)

        def also(k):
            if mode == "z":
                return [((q, "d", u, k), "sibling", size, twice(whole, k))]
            return [((q, "v", u, k), "y_far", size, twice(on, k))]

        def onward(way, step, k):
            return ((q, "g", u, way, step), around_z[way], size, twice(on, k))

        add(("G", q, u), needs, 0.1, settle, [onward(0, 1, 0), onward(1, 1, 0)] + also(0))
        holder = {0: ("G", q, u)}
        for way in range(2):
            for step in (1, 2, 3, 4):
                if step == 4 and way != far:
                    continue
                k = (8 - step) % 8 if way == 0 else step
                further = [onward(way, step + 1, k)] if step < 3 or (step == 3 and way == far) else []
                add(("F", q, u, way, step), [msg("g", u, way, step)], 0.03, None, further + also(k))
                holder[k] = ("F", q, u, way, step)
        if mode == "y":
            for k in range(8):
                add(("V", q, u, k), [msg("v", u, k), holder[k]], 0.02, None,
                    [((q, "d", u, k), "sibling", 2 * size, twice(whole, k))])
                holder[k] = ("V", q, u, k)
        return list(holder.values()), [msg("d", u, k) for k in range(8)]

    for q in range(CHUNKS):
        chunk(q)

    copies, waited = {}, set()
    every = list(tasks)
    for name in [every[i] for i in ORDER]:
        _, needs, _, messages, body = tasks[name]
        for need in needs:
            if need[0] == "m" and need not in waited:
                waited.add(need)
                copies[need[1:]].wait_recv()
        if body is not None:
            body()
        for key, link, _, refs in messages:
            src, dst = refs()
            copy = pltpu.make_async_remote_copy(
                src_ref=src, dst_ref=dst, send_sem=send_sem.at[len(copies)], recv_sem=recv_sem.at[len(copies)],
                device_id=device[link], device_id_type=MESH,
            )
            copy.start()
            copies[key] = copy
    for copy in copies.values():
        copy.wait_send()
    for store in stores:
        store.wait()


def on_device(hamiltonian, vectors):
    n = CHUNKS
    modes = "".join(MODES)
    copies = n * (7 + STREAMS + 4) + 3 * SUMS.count("d") + 23 * modes.count("z") + 38 * modes.count("y")
    return pl.pallas_call(
        kernel,
        out_shape=jax.ShapeDtypeStruct((OWN, n * WIDE), F32),
        in_specs=[pl.BlockSpec(memory_space=pl.ANY)] * 2,
        out_specs=pl.BlockSpec(memory_space=pl.ANY),
        scratch_shapes=[
            pltpu.VMEM((OWN, n * WIDE), F32),
            pltpu.VMEM((n, OWN, WIDE), F32),
            pltpu.VMEM((PIECES, OWN, COLS), F32),
            pltpu.VMEM((ROWS, COLS), BF16),
            pltpu.VMEM((ROWS, COLS), BF16),
            pltpu.VMEM((n, 8, OWN, WIDE), F32),
            pltpu.VMEM((2 * WIDE, ROWS), BF16),
            pltpu.VMEM((n, 2, STREAMS, 8, 2, 8, LANES), F32),
            pltpu.VMEM((n, STREAMS, 8, 2, 8, LANES), F32),
            pltpu.VMEM((n, STREAMS, 8, 8, LANES), F32),
            pltpu.VMEM((n, STREAMS, 2, 4, 2, 8, LANES), F32),
            pltpu.VMEM((n, STREAMS, 2, 8, LANES), F32),
            pltpu.VMEM((n, STREAMS, 2, 8, LANES), F32),
            pltpu.VMEM((n, 2, STREAMS, 8, 2, 8, LANES), F32),
            pltpu.VMEM((2 * WIDE, LANES), BF16),
            pltpu.VMEM((n, 2, 4, OWN, WIDE), F32),
            pltpu.VMEM((n, 3, 2, OWN, WIDE), F32),
            pltpu.VMEM((n, 7, OWN, WIDE), F32),
            pltpu.VMEM((n, 4, OWN, WIDE), F32),
            pltpu.SemaphoreType.DMA,
            pltpu.SemaphoreType.DMA((n,)),
            pltpu.SemaphoreType.DMA((PIECES,)),
            pltpu.SemaphoreType.DMA((copies,)),
            pltpu.SemaphoreType.DMA((copies,)),
        ],
        compiler_params=pltpu.CompilerParams(
            collective_id=0, has_side_effects=True, vmem_limit_bytes=66_000_000
        ),
    )(hamiltonian, vectors)


def solution(mesh):
    return jax.shard_map(
        on_device,
        mesh=mesh,
        in_specs=(P("row", "col"), P(("row", "col"), None)),
        out_specs=P(("row", "col"), None),
        check_vma=False,
    )
```
